512 devices in a mesh: tm: 32 (over z_lo, x), space: 16 (over y, z_hi, core).
Axes of the slice: x: 4, y: 4, z: 16 (z_hi: 2, z_lo: 8; z = z_hi * 8 + z_lo), core: 2. Of those that a mesh axis runs over, the one named last changes fastest.
Arguments:
- states: float32 [32, 8, 24, 128, 128], P('tm', None, None, 'space'), may hold values from -6 to 6
- bio_matrix: float32 [8, 8], replicated, may hold values from -2 to 2
- uptake_rate: float32 [128, 128], P('space'), may hold values from 0.2 to 1
- mixing: float32 [23, 128, 128], P(None, 'space'), may hold values from 0.3 to 10
- land_sea: int32 [128, 128], P('space'), may hold values 0 or 1
- levels_active: int32 [128, 128], P('space'), may hold values from 1 to 24
Outputs:
- state_grad: float32 [32, 8, 24, 128, 128], P('tm', None, None, 'space')
- rate_grad: float32 [128, 128], P('space')
The draws below stay inside these ranges and needn't reach their ends.
All inputs are finite; a program needn't handle non-finite values. No bound on the sum of `land_sea` on one device may be relied on, other than what follows from the above.
Results may differ from the reference program's by a relative error of at most 0.0001.
Values sent between devices are 32-bit elements; how exact they have to be, the bound alone decides.
No kernel may reach another device: no remote copies, remote signals or barrier semaphores. Data moves between devices by JAX's collectives and lax.ppermute only.
A program may use at most 64 MiB of HBM per device.

```python
import math
import jax
import jax.numpy as jnp
from jax import lax

TR = 8
K = 24
KM1 = 23
STEPS = 4
LON = 128
NLAT = 128
SLABS = 32
N_TM = 32


def set_ends(values, key, least, high):
    place = [jax.random.randint(jax.random.fold_in(key, axis), (), 0, length) for axis, length in enumerate(values.shape)]
    longest = values.shape.index(max(values.shape))
    beside = place[:longest] + [(place[longest] + 1) % values.shape[longest]] + place[longest + 1:]
    return values.at[tuple(place)].set(least).at[tuple(beside)].set(high)


def block_scale(key, dims, split, least, largest):
    loudness, own = 1.0, jax.random.fold_in(key, 6)
    for position, blocks in split:
        steps = jnp.exp(jax.random.uniform(jax.random.fold_in(own, position), (blocks,), jnp.float32, least / len(split), largest / len(split)))
        loudness = loudness * jnp.repeat(steps, dims[position] // blocks).reshape([-1 if axis == position else 1 for axis in range(len(dims))])
    return loudness


def gaussian(own_key, shape, spread, most, pieces=(), kind=jnp.bfloat16):
    factor_of = block_scale(own_key, shape, pieces, -0.22, 0.18) if pieces else 1.0
    values = jax.random.normal(own_key, shape, jnp.float32) * spread * factor_of
    return jnp.minimum(jnp.maximum(values, -most), most).astype(kind)


def setup_inputs(seed: int = 0) -> dict:
    splits = jax.random.split(jax.random.key(seed), 7)
    states = gaussian(splits[0], (SLABS, TR, K, NLAT, LON), 1.0, 6.0, ((0, 32), (3, 16)), jnp.float32)
    bio_matrix = gaussian(splits[1], (TR, TR), TR ** -0.5, 2.0, (), jnp.float32)
    uptake_rate = jnp.clip(jnp.exp(math.log(1.0) - 1.609438 * jax.random.uniform(splits[2], (NLAT, LON), jnp.float32) ** block_scale(splits[2], (NLAT, LON), ((0, 16),), -0.2, 0.2)), 0.2, 1.0)
    mixing = jnp.clip(jnp.exp(math.log(10.0) - 3.506558 * jax.random.uniform(splits[3], (KM1, NLAT, LON), jnp.float32) ** block_scale(splits[3], (KM1, NLAT, LON), ((1, 16),), -0.2, 0.2)), 0.3, 10.0)
    land_sea = set_ends((jax.random.randint(splits[4], (NLAT, LON), 0, 5) < 4).astype(jnp.int32), jax.random.fold_in(splits[4], 1), 0, 1)
    levels_active = set_ends(jax.random.randint(splits[5], (NLAT, LON), 1, K + 1), jax.random.fold_in(splits[5], 1), 1, K).astype(jnp.int32)
    return dict(states=states, bio_matrix=bio_matrix, uptake_rate=uptake_rate, mixing=mixing, land_sea=land_sea, levels_active=levels_active)


lateral_mix = 0.24
bio_step = 0.25

def vertical_factors(wet, mixing):
    couple = mixing * wet[:-1] * wet[1:]
    depth = wet.shape[0]
    pivots = []
    for height in range(depth):
        middle = 1.0 + jnp.zeros_like(wet[0])
        if height > 0:
            middle = middle + couple[height - 1]
        if height < depth - 1:
            middle = middle + couple[height]
        if height > 0:
            middle = middle - couple[height - 1] * couple[height - 1] / pivots[-1]
        pivots.append(middle)
    return (couple, pivots)

def column_solve(rhs, couple, pivots):
    depth = rhs.shape[1]
    sweep = [rhs[:, 0] / pivots[0]]
    for height in range(1, depth):
        sweep.append((rhs[:, height] + couple[height - 1] * sweep[-1]) / pivots[height])
    result = [sweep[depth - 1]]
    for height in range(depth - 2, -1, -1):
        result.append(sweep[height] + couple[height] / pivots[height] * result[-1])
    return jnp.stack(result[::-1], axis=1)

def shift_cols(field):
    zero_col = jnp.zeros(field.shape[:-1] + (1,), field.dtype)
    east_val = jnp.concatenate([field[..., 1:], zero_col], axis=-1)
    west_val = jnp.concatenate([zero_col, field[..., :-1]], axis=-1)
    return (east_val, west_val)

def face_factors(wet_pad):
    wet = wet_pad[:, 1:-1]
    east_val, west_val = shift_cols(wet)
    return (wet * wet_pad[:, 2:], wet * wet_pad[:, :-2], wet * east_val, wet * west_val)

def lateral_flux(field, padded, faces):
    east_val, west_val = shift_cols(field)
    total = faces[0] * (padded[:, :, 2:] - field) + faces[1] * (padded[:, :, :-2] - field)
    total = total + faces[2] * (east_val - field) + faces[3] * (west_val - field)
    return lateral_mix * total

def pad_rows(field):
    return jnp.pad(field, ((0, 0), (0, 0), (1, 1), (0, 0)))

def reference(states, bio_matrix, uptake_rate, mixing, land_sea, levels_active):
    heights = jnp.arange(K, dtype=jnp.int32)[:, None, None]
    wet = ((land_sea[None] == 1) & (heights < levels_active[None])).astype(jnp.float32)
    wet_pad = jnp.pad(wet, ((0, 0), (1, 1), (0, 0)))
    faces = face_factors(wet_pad)
    couple, pivots = vertical_factors(wet, mixing)

    def forward(start):
        field = start
        mixes = []
        for step_idx in range(STEPS):
            mixed = jnp.einsum('tu,ukln->tkln', bio_matrix, field, precision=lax.Precision.HIGHEST)
            mixes.append(mixed)
            star = wet * (field + lateral_flux(field, pad_rows(field), faces) + bio_step * uptake_rate * mixed)
            field = column_solve(star, couple, pivots)
        return (field, mixes)
    ends = lax.map(lambda start: forward(start)[0], states)
    defects = ends - wet * jnp.roll(states, -1, axis=0)

    def backward(pair):
        start, defect = pair
        unused, mixes = forward(start)
        lam = defect
        rate_term = jnp.zeros(uptake_rate.shape, jnp.float32)
        for step_idx in range(STEPS - 1, -1, -1):
            lstar = column_solve(lam, couple, pivots)
            rate_term = rate_term + bio_step * lax.optimization_barrier(jnp.sum(lstar * wet * mixes[step_idx], axis=(0, 1)))
            low = wet * lstar
            back_mix = jnp.einsum('tu,tkln->ukln', bio_matrix, low, precision=lax.Precision.HIGHEST)
            lam = low + lateral_flux(low, pad_rows(low), faces) + bio_step * uptake_rate * back_mix
        return (lam, rate_term)
    lams, rate_terms = lax.map(backward, (states, defects))
    state_grad = lams - jnp.roll(defects, 1, axis=0)
    scale = 1.0 / math.sqrt(STEPS * TR * K * N_TM)
    rate_grad = lax.optimization_barrier(jnp.sum(rate_terms, axis=0)) * scale
    return (state_grad, rate_grad)
```

```python
import math

import jax
import jax.numpy as jnp
from jax import lax
from jax.experimental import pallas as pl
from jax.experimental.pallas import tpu as pltpu
from jax.sharding import PartitionSpec as P


TR = 8
K = 24
STEPS = 4
PARTS = (4, 2, 2)
ROWS = 8
LON = 128
HALF = K // 2
QUARTER = K // 4
GEO = 28
GEO_HALF = GEO // 2
GEO_QUARTER = GEO // 4
PACKED = TR * HALF + GEO_HALF
SPLIT = TR * QUARTER + GEO_QUARTER

lateral_mix = 0.24
bio_step = 0.25

DIAG, DOWN, UP, EAST, WEST, BIO, INV, LOWER, BACK, WET = range(10)

VMEM = pl.BlockSpec(memory_space=pltpu.VMEM)
SMEM = pl.BlockSpec(memory_space=pltpu.SMEM)
HBM = pl.BlockSpec(memory_space=pltpu.HBM)


def sublane():
    return lax.broadcasted_iota(jnp.int32, (ROWS, LON), 0)


def pack_pair(even_dev, upper, first, second):
    first_turned, second_turned = pltpu.roll(first, 4, 0), pltpu.roll(second, 4, 0)
    top = jnp.where(upper, first, second_turned)
    bottom = jnp.where(upper, first_turned, second)
    return jnp.where(even_dev, bottom, top), jnp.where(even_dev, top, bottom)


def unpack_pair(even_dev, upper, chip, far):
    below, above = jnp.where(even_dev, chip, far), jnp.where(even_dev, far, chip)
    first = jnp.where(upper, below, pltpu.roll(above, 4, 0))
    second = jnp.where(upper, pltpu.roll(below, 4, 0), above)
    return first, second


def split_rows(even_dev, first, second):
    low = sublane() % 4 < 2
    lows = jnp.where(low, first, pltpu.roll(second, 2, 0))
    highs = jnp.where(low, pltpu.roll(first, ROWS - 2, 0), second)
    return jnp.where(even_dev, lows, highs), jnp.where(even_dev, highs, lows)


def join_rows(even_dev, near, rest):
    low = sublane() % 4 < 2
    lows, highs = jnp.where(even_dev, rest, near), jnp.where(even_dev, near, rest)
    first = jnp.where(low, lows, pltpu.roll(highs, 2, 0))
    second = jnp.where(low, pltpu.roll(lows, ROWS - 2, 0), highs)
    return first, second


def rows_beside(pair):
    row = sublane()
    turned = [pltpu.roll(v, ROWS - 1, 0) for v in pair]
    down = [jnp.where(row == ROWS - 1, turned[1 - i], turned[i]) for i in range(2)]
    turned = [pltpu.roll(v, 1, 0) for v in pair]
    up = [jnp.where(row == 0, turned[1 - i], turned[i]) for i in range(2)]
    return down, up


def cols_beside(v):
    return pltpu.roll(v, LON - 1, 1), pltpu.roll(v, 1, 1)


def pack_kernel(parity, *refs):
    inputs, held, (chip_out, near_out, rest_out), sems = refs[:5], refs[5:10], refs[10:13], refs[13]
    copies = [pltpu.make_async_copy(src, dst, sems.at[n]) for n, (src, dst) in enumerate(zip(inputs, held))]
    for copy in copies:
        copy.start()
    for copy in copies:
        copy.wait()
    x, mixing, rate, land, levels = held
    even_dev = jnp.full((ROWS, LON), parity[0], jnp.int32) == 0
    upper = sublane() < 4

    def pack(tiles, chip_at, far_at):
        chip, far = pack_pair(even_dev, upper, tiles[0], tiles[1])
        chip_next, far_next = pack_pair(even_dev, upper, tiles[2], tiles[3])
        chip_out[chip_at] = chip
        chip_out[chip_at + 1] = chip_next
        near_out[far_at], rest_out[far_at] = split_rows(even_dev, far, far_next)

    @pl.loop(0, QUARTER)
    def _(p):
        for t in range(TR):
            pack([x[t, 4 * p + n] for n in range(4)], t * HALF + 2 * p, t * QUARTER + p)

    depth = jnp.where(land[...] == 1, levels[...], 0).astype(jnp.float32)
    spare = [jnp.zeros_like(depth)] * (GEO - K - 1)
    fields = [mixing[k] for k in range(K - 1)] + [rate[...], depth] + spare
    for p in range(GEO_QUARTER):
        pack(fields[4 * p : 4 * p + 4], TR * HALF + 2 * p, TR * QUARTER + p)


def star(level, c, coef, splat):
    tiles = 2
    k = [[coef[n, level, i] for n in (DIAG, DOWN, UP, EAST, WEST, BIO)] for i in range(tiles)]
    out, own_mixed = [[] for _ in range(tiles)], []
    for t in range(TR):
        down, up = rows_beside([c[0][t], c[1][t]])
        for i in range(tiles):
            mixed = splat[t * TR] * c[i][0]
            for u in range(1, TR):
                mixed = mixed + splat[t * TR + u] * c[i][u]
            east, west = cols_beside(c[i][t])
            diag, fd, fu, fe, fw, bio = k[i]
            out[i].append(diag * c[i][t] + fd * down[i] + fu * up[i] + fe * east + fw * west + bio * mixed)
            if i == 0:
                own_mixed.append(mixed)
    return out, own_mixed


def halo_levels(even_dev, upper, chip_in, chip_at, near_in, rest_in, far_at):
    near = near_in[far_at]
    rest = jnp.zeros_like(near) if rest_in is None else rest_in[far_at]
    first, second = join_rows(even_dev, near, rest)
    return unpack_pair(even_dev, upper, chip_in[chip_at], first) + unpack_pair(
        even_dev, upper, chip_in[chip_at + 1], second
    )


def geometry(even_dev, upper, mixing, rate, land, levels, chip_in, near_in, rest_in, halo, coef):
    for p in range(GEO_QUARTER):
        tiles = halo_levels(even_dev, upper, chip_in, TR * HALF + 2 * p, near_in, rest_in, TR * QUARTER + p)
        for n in range(4):
            halo[4 * p + n] = tiles[n]
    depth = [jnp.where(land[...] == 1, levels[...], 0).astype(jnp.float32), halo[K]]
    speed = [rate[...], halo[K - 1]]
    lane = lax.broadcasted_iota(jnp.int32, (ROWS, LON), 1)
    zero = jnp.zeros((ROWS, LON), jnp.float32)

    def wet_at(k):
        level = jnp.full((ROWS, LON), k, jnp.int32).astype(jnp.float32)
        return [jnp.where(level < depth[i], 1.0, 0.0) for i in range(2)]

    def body(k, carry):
        before, back_before = carry
        wet, wet_below = wet_at(k), wet_at(k + 1)
        down, up = rows_beside(wet)
        at = jnp.minimum(k, K - 2)
        mix = [mixing[at], halo[at]]
        after_list, back_list = [], []
        for i in range(2):
            couple = mix[i] * wet[i] * wet_below[i]
            pivot = 1.0 + before[i] + couple - before[i] * back_before[i]
            inv = 1.0 / pivot
            east, west = cols_beside(wet[i])
            fd, fu = lateral_mix * (wet[i] * down[i]), lateral_mix * (wet[i] * up[i])
            fe = jnp.where(lane == LON - 1, 0.0, lateral_mix * (wet[i] * east))
            fw = jnp.where(lane == 0, 0.0, lateral_mix * (wet[i] * west))
            coef[DIAG, k, i] = wet[i] * (1.0 - (fd + fu + fe + fw))
            coef[DOWN, k, i] = fd
            coef[UP, k, i] = fu
            coef[EAST, k, i] = fe
            coef[WEST, k, i] = fw
            coef[BIO, k, i] = bio_step * speed[i] * wet[i]
            coef[INV, k, i] = inv
            coef[LOWER, k, i] = before[i] * inv
            coef[BACK, k, i] = couple * inv
            coef[WET, k, i] = wet[i]
            after_list.append(couple)
            back_list.append(couple * inv)
        return tuple(after_list), tuple(back_list)

    lax.fori_loop(0, K, body, ((zero, zero), (zero, zero)))


def spread(matrix, splat, transposed):
    for t in range(TR):
        for u in range(TR):
            value = matrix[u, t] if transposed else matrix[t, u]
            splat[t * TR + u] = jnp.full((ROWS, LON), value, jnp.float32)


def place(t):
    part = 0
    while t >= PARTS[part]:
        t, part = t - PARTS[part], part + 1
    return part, t


def load_halo(even_dev, upper, own, chip_in, near_in, rest_in, field):
    @pl.loop(0, QUARTER)
    def _(p):
        for t in range(TR):
            part, at = place(t) if len(own) > 1 else (0, t)
            tiles = halo_levels(even_dev, upper, chip_in, t * HALF + 2 * p, near_in, rest_in, t * QUARTER + p)
            for n in range(4):
                field[4 * p + n, 1, t] = tiles[n]
                field[4 * p + n, 0, t] = own[part][at, 4 * p + n]


def part_kernel(parity, matrix, x, following, mixing, rate, land, levels, chip_in, near_in, rest_out, coef, *work):
    inputs = (parity, matrix, x, following, mixing, rate, land, levels, chip_in, near_in, None)
    forward(inputs, None, None, None, rest_out, None, coef, *work)


def full_kernel(parity, matrix, x, following, mixing, rate, land, levels, chip_in, near_in, rest_in,
                first, second, third, chip_out, near_out, kept, coef, *work):
    inputs = (parity, matrix, x, following, mixing, rate, land, levels, chip_in, near_in, rest_in)
    forward(inputs, (first, second, third), chip_out, near_out, None, kept, coef, *work)


def forward(inputs, defect, chip_out, near_out, rest_out, kept, coef, halo, splat, field, sweep):
    parity, matrix, x, following, mixing, rate, land, levels, chip_in, near_in, rest_in = inputs
    even_dev = jnp.full((ROWS, LON), parity[0], jnp.int32) == 0
    upper = sublane() < 4
    spread(matrix, splat, False)
    geometry(even_dev, upper, mixing, rate, land, levels, chip_in, near_in, rest_in, halo, coef)
    load_halo(even_dev, upper, (x,), chip_in, near_in, rest_in, field)

    for step in range(STEPS):
        tiles = 2 if step < STEPS - 1 else 1

        def down_body(k, carry):
            c = [[field[k, i, t] for t in range(TR)] for i in range(2)]
            out, _ = star(k, c, coef, splat) if tiles == 2 else star_own(k, c, coef, splat)
            result = []
            for i in range(tiles):
                inv, lower = coef[INV, k, i], coef[LOWER, k, i]
                for t in range(TR):
                    value = out[i][t] * inv + lower * carry[i * TR + t]
                    sweep[k, i, t] = value
                    result.append(value)
            return tuple(result)

        zero = jnp.zeros((ROWS, LON), jnp.float32)
        lax.fori_loop(0, K, down_body, (zero,) * (TR * tiles))

        def up_body(j, carry):
            k = K - 1 - j
            result = []
            for i in range(tiles):
                back = coef[BACK, k, i]
                for t in range(TR):
                    value = sweep[k, i, t] + back * carry[i * TR + t]
                    field[k, i, t] = value
                    if kept is not None and i == 0 and step < STEPS - 1:
                        kept[step, k, t] = value
                    result.append(value)
            return tuple(result)

        lax.fori_loop(0, K, up_body, (zero,) * (TR * tiles))

    @pl.loop(0, QUARTER)
    def _(p):
        for t in range(TR):
            tiles = [
                field[4 * p + n, 0, t] - coef[WET, 4 * p + n, 0] * following[t, 4 * p + n] for n in range(4)
            ]
            chip, far = pack_pair(even_dev, upper, tiles[0], tiles[1])
            chip_next, far_next = pack_pair(even_dev, upper, tiles[2], tiles[3])
            near, rest = split_rows(even_dev, far, far_next)
            if rest_out is not None:
                rest_out[t * QUARTER + p] = rest
            else:
                part, at = place(t)
                for n in range(4):
                    defect[part][at, 4 * p + n] = tiles[n]
                chip_out[t * HALF + 2 * p] = chip
                chip_out[t * HALF + 2 * p + 1] = chip_next
                near_out[t * QUARTER + p] = near


def star_own(level, c, coef, splat):
    diag, fd, fu, fe, fw, bio = [coef[n, level, 0] for n in (DIAG, DOWN, UP, EAST, WEST, BIO)]
    row = sublane()
    out, own_mixed = [], []
    for t in range(TR):
        mixed = splat[t * TR] * c[0][0]
        for u in range(1, TR):
            mixed = mixed + splat[t * TR + u] * c[0][u]
        down = jnp.where(row == ROWS - 1, pltpu.roll(c[1][t], ROWS - 1, 0), pltpu.roll(c[0][t], ROWS - 1, 0))
        up = jnp.where(row == 0, pltpu.roll(c[1][t], 1, 0), pltpu.roll(c[0][t], 1, 0))
        east, west = cols_beside(c[0][t])
        out.append(diag * c[0][t] + fd * down + fu * up + fe * east + fw * west + bio * mixed)
        own_mixed.append(mixed)
    return [out], own_mixed


def backward_kernel(parity, matrix, x, kept, coef, first, second, third, chip_in, near_in, rest_in,
                    lam_out, rate_out, splat, field, sweep):
    even_dev = jnp.full((ROWS, LON), parity[0], jnp.int32) == 0
    upper = sublane() < 4
    spread(matrix, splat, True)

    load_halo(even_dev, upper, (first, second, third), chip_in, near_in, rest_in, field)
    zero = jnp.zeros((ROWS, LON), jnp.float32)
    total = zero
    for step in range(STEPS - 1, -1, -1):

        def down_body(k, carry):
            result = []
            for i in range(2):
                inv, lower = coef[INV, k, i], coef[LOWER, k, i]
                for t in range(TR):
                    value = field[k, i, t] * inv + lower * carry[i * TR + t]
                    sweep[k, i, t] = value
                    result.append(value)
            return tuple(result)

        lax.fori_loop(0, K, down_body, (zero,) * (TR * 2))

        def up_body(j, carry):
            k = K - 1 - j
            low = [[], []]
            for i in range(2):
                back = coef[BACK, k, i]
                for t in range(TR):
                    low[i].append(sweep[k, i, t] + back * carry[i * TR + t])
            if step > 0:
                out, mixed = star(k, low, coef, splat)
                for i in range(2):
                    for t in range(TR):
                        field[k, i, t] = out[i][t]
            else:
                out, mixed = star_own(k, low, coef, splat)
                for t in range(TR):
                    lam_out[t, k] = out[0][t]
            old = [kept[step - 1, k, t] if step > 0 else x[t, k] for t in range(TR)]
            term = old[0] * mixed[0]
            for t in range(1, TR):
                term = term + old[t] * mixed[t]
            return tuple(low[0] + low[1]) + (carry[-1] + coef[WET, k, 0] * term,)

        total = lax.fori_loop(0, K, up_body, (zero,) * (TR * 2) + (total,))[-1]
    rate_out[...] = bio_step * total


def shape(*dims):
    return jax.ShapeDtypeStruct(dims, jnp.float32)


def scratch(*dims):
    return pltpu.VMEM(dims, jnp.float32)


def call(kernel, scalars, arrays, outs, scratches, where=VMEM):
    return pl.pallas_call(
        kernel,
        out_shape=outs,
        in_specs=[SMEM] * len(scalars) + [where] * len(arrays),
        out_specs=tuple(VMEM for _ in outs),
        scratch_shapes=scratches,
        compiler_params=pltpu.CompilerParams(vmem_limit_bytes=48 << 20),
    )(*scalars, *arrays)


def shifted(block, axis, distance):
    count = lax.axis_size(axis)
    return lax.ppermute(block, axis, [((i - distance) % count, i) for i in range(count)])


def swap_chip(block):
    return lax.ppermute(block, "space", [(i, i ^ 1) for i in range(lax.axis_size("space"))])


def swap_far(block):
    pairs = [(i, i + 1) for i in range(1, lax.axis_size("space") - 1, 2)]
    return lax.ppermute(block, "space", pairs + [(j, i) for i, j in pairs])


def swapped(value, mask):
    return lax.ppermute(value, "tm", [(i, i ^ mask) for i in range(lax.axis_size("tm"))])


def per_device(states, bio_matrix, uptake_rate, mixing, land_sea, levels_active):
    own = states[0]
    parity = (lax.axis_index("space") % 2).astype(jnp.int32).reshape(1)
    fields = (mixing, uptake_rate, land_sea, levels_active)
    following = shifted(own, "tm", -1)
    given = tuple(pltpu.with_memory_space_constraint(array, pltpu.HBM) for array in (own,) + fields)
    own, *fields, chip_send, near_send, rest_send = call(
        pack_kernel,
        (parity,),
        given,
        tuple(jax.ShapeDtypeStruct(array.shape, array.dtype) for array in given)
        + (shape(PACKED, ROWS, LON), shape(SPLIT, ROWS, LON), shape(SPLIT, ROWS, LON)),
        [pltpu.SemaphoreType.DMA((5,))],
        HBM,
    )
    fields = tuple(fields)
    chip = swap_chip(chip_send)
    near = swap_far(near_send)
    rest = swap_far(rest_send)
    work = [scratch(TR * TR, ROWS, LON), scratch(K, 2, TR, ROWS, LON), scratch(K, 2, TR, ROWS, LON)]
    halo = scratch(GEO, ROWS, LON)
    (rest_send,) = call(
        part_kernel,
        (parity, bio_matrix),
        (own, following) + fields + (chip, near),
        (shape(TR * QUARTER, ROWS, LON),),
        [scratch(10, K, 2, ROWS, LON), halo] + work,
    )
    rest_defect = swap_far(rest_send)
    first, second, third, chip_send, near_send, kept, coef = call(
        full_kernel,
        (parity, bio_matrix),
        (own, following) + fields + (chip, near, rest),
        (
            *[shape(tracers, K, ROWS, LON) for tracers in PARTS],
            shape(TR * HALF, ROWS, LON),
            shape(TR * QUARTER, ROWS, LON),
            shape(STEPS - 1, K, TR, ROWS, LON),
            shape(10, K, 2, ROWS, LON),
        ),
        [halo] + work,
    )
    near_defect = swap_far(near_send)
    chip_defect = swap_chip(chip_send)
    lam, rate_term = call(
        backward_kernel,
        (parity, bio_matrix),
        (own, kept, coef, first, second, third, chip_defect, near_defect, rest_defect),
        (shape(TR, K, ROWS, LON), shape(ROWS, LON)),
        work,
    )
    rate_sum = rate_term + swapped(rate_term, 16)
    earlier_first = shifted(first, "tm", 1)
    rate_sum = rate_sum + swapped(rate_sum, 8)
    earlier_second = shifted(second, "tm", 1)
    rate_sum = rate_sum + swapped(rate_sum, 4)
    earlier_third = shifted(third, "tm", 1)
    for mask in (2, 1):
        rate_sum = rate_sum + swapped(rate_sum, mask)
    scale = 1.0 / math.sqrt(STEPS * TR * K * lax.axis_size("tm"))
    earlier = jnp.concatenate([earlier_first, earlier_second, earlier_third], axis=0)
    return ((lam - earlier)[None], rate_sum * scale)


def ordered(mesh, body, in_specs, out_specs):
    return jax.shard_map(body, mesh=mesh, in_specs=in_specs, out_specs=out_specs, check_vma=False)


def solution(mesh):
    return ordered(
        mesh,
        per_device,
        (
            P("tm", None, None, "space", None),
            P(),
            P("space", None),
            P(None, "space", None),
            P("space", None),
            P("space", None),
        ),
        (P("tm", None, None, "space", None), P("space", None)),
    )
```

```python
import math

import jax
import jax.numpy as jnp
from jax import lax
from jax.experimental import pallas as pl
from jax.experimental.pallas import tpu as pltpu
from jax.sharding import PartitionSpec as P


TR = 8
K = 24
STEPS = 4
ROWS = 8
LON = 128
HALF = K // 2
QUARTER = K // 4
GEO = 28
GEO_HALF = GEO // 2
GEO_QUARTER = GEO // 4
PACKED = TR * HALF + GEO_HALF
SPLIT = TR * QUARTER + GEO_QUARTER

lateral_mix = 0.24
bio_step = 0.25

DIAG, DOWN, UP, EAST, WEST, BIO, INV, LOWER, BACK, WET = range(10)


VMEM = pl.BlockSpec(memory_space=pltpu.VMEM)
SMEM = pl.BlockSpec(memory_space=pltpu.SMEM)
HBM = pl.BlockSpec(memory_space=pltpu.HBM)


def sublane():
    return lax.broadcasted_iota(jnp.int32, (ROWS, LON), 0)


def pack_pair(even_dev, upper, first, second):
    first_turned, second_turned = pltpu.roll(first, 4, 0), pltpu.roll(second, 4, 0)
    top = jnp.where(upper, first, second_turned)
    bottom = jnp.where(upper, first_turned, second)
    return jnp.where(even_dev, bottom, top), jnp.where(even_dev, top, bottom)


def unpack_pair(even_dev, upper, chip, far):
    below, above = jnp.where(even_dev, chip, far), jnp.where(even_dev, far, chip)
    first = jnp.where(upper, below, pltpu.roll(above, 4, 0))
    second = jnp.where(upper, pltpu.roll(below, 4, 0), above)
    return first, second


def split_rows(even_dev, first, second):
    low = sublane() % 4 < 2
    lows = jnp.where(low, first, pltpu.roll(second, 2, 0))
    highs = jnp.where(low, pltpu.roll(first, ROWS - 2, 0), second)
    return jnp.where(even_dev, lows, highs), jnp.where(even_dev, highs, lows)


def join_rows(even_dev, near, rest):
    low = sublane() % 4 < 2
    lows, highs = jnp.where(even_dev, rest, near), jnp.where(even_dev, near, rest)
    first = jnp.where(low, lows, pltpu.roll(highs, 2, 0))
    second = jnp.where(low, pltpu.roll(lows, ROWS - 2, 0), highs)
    return first, second


def rows_beside(pair):
    row = sublane()
    turned = [pltpu.roll(v, ROWS - 1, 0) for v in pair]
    down = [jnp.where(row == ROWS - 1, turned[1 - i], turned[i]) for i in range(2)]
    turned = [pltpu.roll(v, 1, 0) for v in pair]
    up = [jnp.where(row == 0, turned[1 - i], turned[i]) for i in range(2)]
    return down, up


def cols_beside(v):
    return pltpu.roll(v, LON - 1, 1), pltpu.roll(v, 1, 1)


def pack_kernel(parity, *refs):
    inputs, held, (chip_out, near_out, rest_out), sems = refs[:5], refs[5:11], refs[11:14], refs[14]
    halves = (inputs[0].at[pl.ds(0, TR // 2)], inputs[0].at[pl.ds(TR // 2, TR // 2)])
    sources = halves + tuple(inputs[1:])
    copies = [pltpu.make_async_copy(src, dst, sems.at[n]) for n, (src, dst) in enumerate(zip(sources, held))]
    for copy in copies:
        copy.start()
    for copy in copies:
        copy.wait()
    low_half, high_half, mixing, rate, land, levels = held
    x = (low_half, high_half)
    even_dev = jnp.full((ROWS, LON), parity[0], jnp.int32) == 0
    upper = sublane() < 4

    def pack(tiles, chip_at, far_at):
        chip, far = pack_pair(even_dev, upper, tiles[0], tiles[1])
        chip_next, far_next = pack_pair(even_dev, upper, tiles[2], tiles[3])
        chip_out[chip_at] = chip
        chip_out[chip_at + 1] = chip_next
        near_out[far_at], rest_out[far_at] = split_rows(even_dev, far, far_next)

    @pl.loop(0, QUARTER)
    def _(p):
        for t in range(TR):
            pack([x[t // 4][t % 4, 4 * p + n] for n in range(4)], t * HALF + 2 * p, t * QUARTER + p)

    depth = jnp.where(land[...] == 1, levels[...], 0).astype(jnp.float32)
    spare = [jnp.zeros_like(depth)] * (GEO - K - 1)
    fields = [mixing[k] for k in range(K - 1)] + [rate[...], depth] + spare
    for p in range(GEO_QUARTER):
        pack(fields[4 * p : 4 * p + 4], TR * HALF + 2 * p, TR * QUARTER + p)


def star(level, c, coef, splat):
    tiles = 2
    k = [[coef[n, level, i] for n in (DIAG, DOWN, UP, EAST, WEST, BIO)] for i in range(tiles)]
    out, own_mixed = [[] for _ in range(tiles)], []
    for t in range(TR):
        down, up = rows_beside([c[0][t], c[1][t]])
        for i in range(tiles):
            mixed = splat[t * TR] * c[i][0]
            for u in range(1, TR):
                mixed = mixed + splat[t * TR + u] * c[i][u]
            east, west = cols_beside(c[i][t])
            diag, fd, fu, fe, fw, bio = k[i]
            out[i].append(diag * c[i][t] + fd * down[i] + fu * up[i] + fe * east + fw * west + bio * mixed)
            if i == 0:
                own_mixed.append(mixed)
    return out, own_mixed


def halo_levels(even_dev, upper, chip_in, chip_at, near_in, rest_in, far_at):
    near = near_in[far_at]
    rest = jnp.zeros_like(near) if rest_in is None else rest_in[far_at]
    first, second = join_rows(even_dev, near, rest)
    return unpack_pair(even_dev, upper, chip_in[chip_at], first) + unpack_pair(
        even_dev, upper, chip_in[chip_at + 1], second
    )


def geometry(even_dev, upper, mixing, rate, land, levels, chip_in, near_in, rest_in, halo, coef):
    for p in range(GEO_QUARTER):
        tiles = halo_levels(even_dev, upper, chip_in, TR * HALF + 2 * p, near_in, rest_in, TR * QUARTER + p)
        for n in range(4):
            halo[4 * p + n] = tiles[n]
    depth = [jnp.where(land[...] == 1, levels[...], 0).astype(jnp.float32), halo[K]]
    speed = [rate[...], halo[K - 1]]
    lane = lax.broadcasted_iota(jnp.int32, (ROWS, LON), 1)
    zero = jnp.zeros((ROWS, LON), jnp.float32)

    def wet_at(k):
        level = jnp.full((ROWS, LON), k, jnp.int32).astype(jnp.float32)
        return [jnp.where(level < depth[i], 1.0, 0.0) for i in range(2)]

    def body(k, carry):
        before, back_before = carry
        wet, wet_below = wet_at(k), wet_at(k + 1)
        down, up = rows_beside(wet)
        at = jnp.minimum(k, K - 2)
        mix = [mixing[at], halo[at]]
        after_list, back_list = [], []
        for i in range(2):
            couple = mix[i] * wet[i] * wet_below[i]
            pivot = 1.0 + before[i] + couple - before[i] * back_before[i]
            inv = 1.0 / pivot
            east, west = cols_beside(wet[i])
            fd, fu = lateral_mix * (wet[i] * down[i]), lateral_mix * (wet[i] * up[i])
            fe = jnp.where(lane == LON - 1, 0.0, lateral_mix * (wet[i] * east))
            fw = jnp.where(lane == 0, 0.0, lateral_mix * (wet[i] * west))
            coef[DIAG, k, i] = wet[i] * (1.0 - (fd + fu + fe + fw))
            coef[DOWN, k, i] = fd
            coef[UP, k, i] = fu
            coef[EAST, k, i] = fe
            coef[WEST, k, i] = fw
            coef[BIO, k, i] = bio_step * speed[i] * wet[i]
            coef[INV, k, i] = inv
            coef[LOWER, k, i] = before[i] * inv
            coef[BACK, k, i] = couple * inv
            coef[WET, k, i] = wet[i]
            after_list.append(couple)
            back_list.append(couple * inv)
        return tuple(after_list), tuple(back_list)

    lax.fori_loop(0, K, body, ((zero, zero), (zero, zero)))


def spread(matrix, splat, transposed):
    for t in range(TR):
        for u in range(TR):
            value = matrix[u, t] if transposed else matrix[t, u]
            splat[t * TR + u] = jnp.full((ROWS, LON), value, jnp.float32)


def load_halo(even_dev, upper, own, chip_in, near_in, rest_in, field):
    @pl.loop(0, QUARTER)
    def _(p):
        for t in range(TR):
            tiles = halo_levels(even_dev, upper, chip_in, t * HALF + 2 * p, near_in, rest_in, t * QUARTER + p)
            for n in range(4):
                field[4 * p + n, 1, t] = tiles[n]
                field[4 * p + n, 0, t] = own[t * len(own) // TR][t % (TR // len(own)), 4 * p + n]


def part_kernel(parity, matrix, low_half, high_half, main, low_wrap, high_wrap, mixing, rate, land, levels, chip_in, near_in, rest_out, coef, *work):
    x, following = (low_half, high_half), (main, low_wrap, high_wrap)
    inputs = (parity, matrix, x, following, mixing, rate, land, levels, chip_in, near_in, None)
    forward(inputs, None, None, None, rest_out, None, coef, *work)


def full_kernel(parity, matrix, low_half, high_half, main, low_wrap, high_wrap, mixing, rate, land, levels, chip_in, near_in, rest_in,
                defect, first_half, second_half, chip_out, near_out, kept, coef, *work):
    x, following = (low_half, high_half), (main, low_wrap, high_wrap)
    inputs = (parity, matrix, x, following, mixing, rate, land, levels, chip_in, near_in, rest_in)
    forward(inputs, (defect, first_half, second_half), chip_out, near_out, None, kept, coef, *work)


def forward(inputs, defect, chip_out, near_out, rest_out, kept, coef, halo, splat, field, sweep):
    parity, matrix, x, following, mixing, rate, land, levels, chip_in, near_in, rest_in = inputs
    even_dev = jnp.full((ROWS, LON), parity[0], jnp.int32) == 0
    upper = sublane() < 4
    spread(matrix, splat, False)
    geometry(even_dev, upper, mixing, rate, land, levels, chip_in, near_in, rest_in, halo, coef)
    load_halo(even_dev, upper, x, chip_in, near_in, rest_in, field)

    for step in range(STEPS):
        tiles = 2 if step < STEPS - 1 else 1

        def down_body(k, carry):
            c = [[field[k, i, t] for t in range(TR)] for i in range(2)]
            out, _ = star(k, c, coef, splat) if tiles == 2 else star_own(k, c, coef, splat)
            result = []
            for i in range(tiles):
                inv, lower = coef[INV, k, i], coef[LOWER, k, i]
                for t in range(TR):
                    value = out[i][t] * inv + lower * carry[i * TR + t]
                    sweep[k, i, t] = value
                    result.append(value)
            return tuple(result)

        zero = jnp.zeros((ROWS, LON), jnp.float32)
        lax.fori_loop(0, K, down_body, (zero,) * (TR * tiles))

        def up_body(j, carry):
            k = K - 1 - j
            result = []
            for i in range(tiles):
                back = coef[BACK, k, i]
                for t in range(TR):
                    value = sweep[k, i, t] + back * carry[i * TR + t]
                    field[k, i, t] = value
                    if kept is not None and i == 0 and step < STEPS - 1:
                        kept[step, k, t] = value
                    result.append(value)
            return tuple(result)

        lax.fori_loop(0, K, up_body, (zero,) * (TR * tiles))

    @pl.loop(0, QUARTER)
    def _(p):
        for t in range(TR):
            tiles = [
                field[4 * p + n, 0, t]
                - coef[WET, 4 * p + n, 0]
                * (following[0][t, 4 * p + n] + following[1 + t // 4][t % 4, 4 * p + n])
                for n in range(4)
            ]
            chip, far = pack_pair(even_dev, upper, tiles[0], tiles[1])
            chip_next, far_next = pack_pair(even_dev, upper, tiles[2], tiles[3])
            near, rest = split_rows(even_dev, far, far_next)
            if rest_out is not None:
                rest_out[t * QUARTER + p] = rest
            else:
                for n in range(4):
                    defect[0][t, 4 * p + n] = tiles[n]
                    defect[1 + t // 4][t % 4, 4 * p + n] = tiles[n]
                chip_out[t * HALF + 2 * p] = chip
                chip_out[t * HALF + 2 * p + 1] = chip_next
                near_out[t * QUARTER + p] = near


def star_own(level, c, coef, splat):
    diag, fd, fu, fe, fw, bio = [coef[n, level, 0] for n in (DIAG, DOWN, UP, EAST, WEST, BIO)]
    row = sublane()
    out, own_mixed = [], []
    for t in range(TR):
        mixed = splat[t * TR] * c[0][0]
        for u in range(1, TR):
            mixed = mixed + splat[t * TR + u] * c[0][u]
        down = jnp.where(row == ROWS - 1, pltpu.roll(c[1][t], ROWS - 1, 0), pltpu.roll(c[0][t], ROWS - 1, 0))
        up = jnp.where(row == 0, pltpu.roll(c[1][t], 1, 0), pltpu.roll(c[0][t], 1, 0))
        east, west = cols_beside(c[0][t])
        out.append(diag * c[0][t] + fd * down + fu * up + fe * east + fw * west + bio * mixed)
        own_mixed.append(mixed)
    return [out], own_mixed


def backward_kernel(parity, matrix, low_half, high_half, kept, coef, defect, chip_in, near_in, rest_in,
                    lam_out, rate_out, splat, field, sweep):
    even_dev = jnp.full((ROWS, LON), parity[0], jnp.int32) == 0
    upper = sublane() < 4
    spread(matrix, splat, True)

    load_halo(even_dev, upper, (defect,), chip_in, near_in, rest_in, field)
    zero = jnp.zeros((ROWS, LON), jnp.float32)
    total = zero
    for step in range(STEPS - 1, -1, -1):

        def down_body(k, carry):
            result = []
            for i in range(2):
                inv, lower = coef[INV, k, i], coef[LOWER, k, i]
                for t in range(TR):
                    value = field[k, i, t] * inv + lower * carry[i * TR + t]
                    sweep[k, i, t] = value
                    result.append(value)
            return tuple(result)

        lax.fori_loop(0, K, down_body, (zero,) * (TR * 2))

        def up_body(j, carry):
            k = K - 1 - j
            low = [[], []]
            for i in range(2):
                back = coef[BACK, k, i]
                for t in range(TR):
                    low[i].append(sweep[k, i, t] + back * carry[i * TR + t])
            if step > 0:
                out, mixed = star(k, low, coef, splat)
                for i in range(2):
                    for t in range(TR):
                        field[k, i, t] = out[i][t]
            else:
                out, mixed = star_own(k, low, coef, splat)
                for t in range(TR):
                    lam_out[t, k] = out[0][t]
            old = [kept[step - 1, k, t] if step > 0 else (low_half, high_half)[t // 4][t % 4, k] for t in range(TR)]
            term = old[0] * mixed[0]
            for t in range(1, TR):
                term = term + old[t] * mixed[t]
            return tuple(low[0] + low[1]) + (carry[-1] + coef[WET, k, 0] * term,)

        total = lax.fori_loop(0, K, up_body, (zero,) * (TR * 2) + (total,))[-1]
    rate_out[...] = bio_step * total


def shape(*dims):
    return jax.ShapeDtypeStruct(dims, jnp.float32)


def scratch(*dims):
    return pltpu.VMEM(dims, jnp.float32)


def call(kernel, scalars, arrays, outs, scratches, where=VMEM):
    return pl.pallas_call(
        kernel,
        out_shape=outs,
        in_specs=[SMEM] * len(scalars) + [where] * len(arrays),
        out_specs=tuple(VMEM for _ in outs),
        scratch_shapes=scratches,
        compiler_params=pltpu.CompilerParams(vmem_limit_bytes=24 << 20),
    )(*scalars, *arrays)


def moved(block, slabs, distance):
    count = lax.axis_size("tm")
    return lax.ppermute(block, "tm", [(t, (t - distance) % count) for t in range(count) if t % 4 in slabs])


def shifted_to_next(block, wraps):
    count = lax.axis_size("tm")
    pairs = [(t, (t + 1) % count) for t in range(count)]
    return lax.ppermute(block, "tm", [(t, after) for t, after in pairs if (after % 4 == 0) == wraps])


def swap_chip(block):
    return lax.ppermute(block, "space", [(i, i ^ 1) for i in range(lax.axis_size("space"))])


def swap_far(block):
    pairs = [(i, i + 1) for i in range(1, lax.axis_size("space") - 1, 2)]
    return lax.ppermute(block, "space", pairs + [(j, i) for i, j in pairs])


def swapped(value, mask):
    return lax.ppermute(value, "tm", [(i, i ^ mask) for i in range(lax.axis_size("tm"))])


def per_device(states, bio_matrix, uptake_rate, mixing, land_sea, levels_active):
    own = states[0]
    parity = (lax.axis_index("space") % 2).astype(jnp.int32).reshape(1)
    fields = (mixing, uptake_rate, land_sea, levels_active)
    main = moved(own, (1, 2, 3), 1)
    given = tuple(pltpu.with_memory_space_constraint(array, pltpu.HBM) for array in (own,) + fields)
    half = shape(TR // 2, K, ROWS, LON)
    low_half, high_half, *fields, chip_send, near_send, rest_send = call(
        pack_kernel,
        (parity,),
        given,
        (half, half)
        + tuple(jax.ShapeDtypeStruct(array.shape, array.dtype) for array in given[1:])
        + (shape(PACKED, ROWS, LON), shape(SPLIT, ROWS, LON), shape(SPLIT, ROWS, LON)),
        [pltpu.SemaphoreType.DMA((6,))],
        HBM,
    )
    fields = tuple(fields)
    chip = swap_chip(chip_send)
    pairs = [half[n : n + 2] for half in (low_half, high_half) for n in (0, 2)]
    aside = [moved(pairs[x], (0,), -x) for x in (1, 2, 3)]
    near = swap_far(near_send)
    wraps = [moved(pairs[0], (0,), 1)]
    wraps += [moved(block, (x,), x + 1) for x, block in zip((1, 2, 3), aside)]
    low_wrap, high_wrap = jnp.concatenate(wraps[:2]), jnp.concatenate(wraps[2:])
    rest = swap_far(rest_send)
    work = [scratch(TR * TR, ROWS, LON), scratch(K, 2, TR, ROWS, LON), scratch(K, 2, TR, ROWS, LON)]
    halo = scratch(GEO, ROWS, LON)
    (rest_send,) = call(
        part_kernel,
        (parity, bio_matrix),
        (low_half, high_half, main, low_wrap, high_wrap) + fields + (chip, near),
        (shape(TR * QUARTER, ROWS, LON),),
        [scratch(10, K, 2, ROWS, LON), halo] + work,
    )
    rest_defect = swap_far(rest_send)
    defect, first_half, second_half, chip_send, near_send, kept, coef = call(
        full_kernel,
        (parity, bio_matrix),
        (low_half, high_half, main, low_wrap, high_wrap) + fields + (chip, near, rest),
        (
            shape(TR, K, ROWS, LON),
            shape(TR // 2, K, ROWS, LON),
            shape(TR // 2, K, ROWS, LON),
            shape(TR * HALF, ROWS, LON),
            shape(TR * QUARTER, ROWS, LON),
            shape(STEPS - 1, K, TR, ROWS, LON),
            shape(10, K, 2, ROWS, LON),
        ),
        [halo] + work,
    )
    near_defect = swap_far(near_send)
    chip_defect = swap_chip(chip_send)
    earlier = shifted_to_next(defect, False)
    lam, rate_term = call(
        backward_kernel,
        (parity, bio_matrix),
        (low_half, high_half, kept, coef, defect, chip_defect, near_defect, rest_defect),
        (shape(TR, K, ROWS, LON), shape(ROWS, LON)),
        work,
    )
    rate_sum = rate_term + swapped(rate_term, 16)
    wrap_first = shifted_to_next(first_half, True)
    rate_sum = rate_sum + swapped(rate_sum, 8)
    wrap_second = shifted_to_next(second_half, True)
    for mask in (4, 1, 2):
        rate_sum = rate_sum + swapped(rate_sum, mask)
    scale = 1.0 / math.sqrt(STEPS * TR * K * lax.axis_size("tm"))
    earlier = earlier + jnp.concatenate([wrap_first, wrap_second], axis=0)
    return ((lam - earlier)[None], rate_sum * scale)


def ordered(mesh, body, in_specs, out_specs):
    return jax.shard_map(body, mesh=mesh, in_specs=in_specs, out_specs=out_specs, check_vma=False)


def solution(mesh):
    return ordered(
        mesh,
        per_device,
        (
            P("tm", None, None, "space", None),
            P(),
            P("space", None),
            P(None, "space", None),
            P("space", None),
            P("space", None),
        ),
        (P("tm", None, None, "space", None), P("space", None)),
    )
```
